32 devices in a mesh: group: 1, dev: 32 (over z, y, x, core).
Axes of the slice: x: 2, y: 2, z: 4, core: 2. Of those that a mesh axis runs over, the one named last changes fastest.
Arguments:
- traces: bfloat16 [2048, 1024], P(('group', 'dev')), may hold values from -6 to 6
- fetch_rows: int32 [1, 32768], P('group', 'dev'), may hold values from 0 to 2047, as said below
- pair_left: int32 [1, 1024, 32], P('group', 'dev'), may hold values from 0 to 1023
- pair_right: int32 [1, 1024, 32], P('group', 'dev'), may hold values from 0 to 1023
- taper_index: int32 [1, 1024, 32], P('group', 'dev'), may hold values from 0 to 15
- taper_table: float32 [16], replicated, may hold values from 0.1 to 1
Outputs:
- predicted: float32 [1024, 1024], P('dev', 'group')
The draws below stay inside these ranges and needn't reach their ends.
Inputs may be any that keep to these rules, and one draw needn't show every extreme that they name: `fetch_rows`: entry j of device d's block of 1024 entries (columns d * 1024 to (d + 1) * 1024 - 1) names a trace held by device j // 32 of the group: it lies in [(j // 32) * 64, (j // 32 + 1) * 64). So every device lists exactly 32 traces of each device of its group.
All inputs are finite; a program needn't handle non-finite values.
Results may differ from the reference program's by a relative error of at most 0.0003.
Values may be sent and summed in bfloat16 or wider, within the bound.
No kernel may reach another device: no remote copies, remote signals or barrier semaphores. Data moves between devices by JAX's collectives and lax.ppermute only.
A program may use at most 64 MiB of HBM per device.

```python
import math
import jax
import jax.numpy as jnp
from jax import lax

NT = 1024
APERTURE = 32
TAPERS = 16
OUT_DEV = 32
TR_DEV = 64
FETCH_DEV = 1024
GROUPS = 1
OUTS = 1024
TRACES = 2048
FETCHES = 32768
PER_OWNER = 32
N_GROUP = 1
N_DEV = 32


def draw_fetch_rows(key, part):
    column = jnp.arange(FETCHES, dtype=jnp.int32)
    owner_index = column % FETCH_DEV // PER_OWNER
    offset = jax.random.randint(key, (GROUPS, FETCHES), 0, TR_DEV, dtype=jnp.int32)
    return (owner_index[None, :] * TR_DEV + offset).astype(jnp.int32)


def set_ends(drawn, key, low, high):
    extent = drawn.shape
    place = [jax.random.randint(jax.random.fold_in(key, axis), (), 0, extent[axis]) for axis in range(len(extent))]
    drawn = drawn.at[tuple(place)].set(low)
    longest = extent.index(max(extent))
    place[longest] = (place[longest] + 1) % extent[longest]
    return drawn.at[tuple(place)].set(high)


def block_levels(own_key, extent, pieces, least, largest):
    def one(position, shards_of):
        steps = jax.random.uniform(jax.random.fold_in(jax.random.fold_in(own_key, 6), position), (shards_of,), jnp.float32, least / len(pieces), largest / len(pieces))
        return jnp.repeat(jnp.exp(steps), extent[position] // shards_of).reshape((-1,) + (1,) * (len(extent) - position - 1))

    loudness = one(*pieces[0])
    for cut in pieces[1:]:
        loudness = loudness * one(*cut)
    return loudness


def normal_values(rng, dims, deviation, most, shards=(), held_as=jnp.bfloat16):
    drawn = deviation * jax.random.normal(rng, dims, jnp.float32)
    if shards:
        drawn = drawn * block_levels(rng, dims, shards, -0.22, 0.18)
    return jnp.clip(drawn, -most, most).astype(held_as)


def setup_inputs(seed: int = 0) -> dict:
    arg_keys = jax.random.split(jax.random.key(seed), 7)
    return {
        "traces": normal_values(arg_keys[0], (TRACES, NT), 1.0, 6.0, ((0, 32),)),
        "fetch_rows": draw_fetch_rows(jax.random.fold_in(arg_keys[6], 71), 0),
        "pair_left": set_ends(jax.random.randint(arg_keys[2], (GROUPS, OUTS, APERTURE), 0, FETCH_DEV), jax.random.fold_in(arg_keys[2], 1), 0, FETCH_DEV - 1).astype(jnp.int32),
        "pair_right": set_ends(jax.random.randint(arg_keys[3], (GROUPS, OUTS, APERTURE), 0, FETCH_DEV), jax.random.fold_in(arg_keys[3], 1), 0, FETCH_DEV - 1).astype(jnp.int32),
        "taper_index": set_ends(jax.random.randint(arg_keys[4], (GROUPS, OUTS, APERTURE), 0, TAPERS), jax.random.fold_in(arg_keys[4], 1), 0, TAPERS - 1).astype(jnp.int32),
        "taper_table": jnp.clip(jnp.exp(jax.random.uniform(arg_keys[5], (TAPERS,), jnp.float32, math.log(0.1), math.log(1.0))), 0.1, 1.0),
    }


def reference(traces, fetch_rows, pair_left, pair_right, taper_index, taper_table):
    weights_all = taper_table[taper_index]

    def one_block(block_index):
        group_index = block_index // N_DEV
        device_index = block_index % N_DEV
        wanted = lax.dynamic_slice_in_dim(fetch_rows[group_index], device_index * FETCH_DEV, FETCH_DEV, 0)
        fetched = jnp.take(traces, wanted + group_index * (TR_DEV * N_DEV), axis=0)
        spectra = jnp.fft.rfft(fetched.astype(jnp.float32), n=2 * NT, axis=1)
        left_rows = lax.dynamic_slice_in_dim(pair_left[group_index], device_index * OUT_DEV, OUT_DEV, 0)
        right_rows = lax.dynamic_slice_in_dim(pair_right[group_index], device_index * OUT_DEV, OUT_DEV, 0)
        weights = lax.dynamic_slice_in_dim(weights_all[group_index], device_index * OUT_DEV, OUT_DEV, 0)
        products = jnp.take(spectra, left_rows, axis=0) * jnp.take(spectra, right_rows, axis=0)
        summed = lax.optimization_barrier(jnp.sum(products * weights[:, :, None], axis=1))
        return jnp.fft.irfft(summed, n=2 * NT, axis=1)[:, :NT].astype(jnp.float32)
    blocks = lax.map(one_block, jnp.arange(N_GROUP * N_DEV, dtype=jnp.int32))
    combined = lax.optimization_barrier(jnp.sum(blocks.reshape(N_GROUP, N_DEV * OUT_DEV, NT), axis=0))
    scaling = 1.0 / jnp.sqrt(jnp.float32(NT * APERTURE * N_GROUP))
    return (combined * scaling).astype(jnp.float32)
```

```python
import functools

import jax
import jax.numpy as jnp
from jax import lax
from jax.experimental import pallas as pl
from jax.experimental.pallas import tpu as pltpu
from jax.sharding import PartitionSpec as P


LANES = 128
ROWS = 8
PER_STEP = 8


def exchange(value, count, even, odd=None):
    odd = even if odd is None else odd
    return lax.ppermute(value, "dev", [(i, i ^ (odd if i & 1 else even)) for i in range(count)])


def gather_blocks(own, count):
    levels = {0: own}
    pieces = []

    def level_of(level):
        if level not in levels:
            low = level & -level
            levels[level] = exchange(level_of(level ^ low), count, 8 * low)
        return levels[level]

    for level in range(count // 8):
        near = exchange(level_of(level), count, 2, 4)
        both = jnp.concatenate([level_of(level), near], axis=0)
        far = exchange(both, count, 4, 2)
        pieces.append((both, 4 * level))
        pieces.append((far, 4 * level + 2))
        pieces.append((exchange(both, count, 1), count // 2 + 4 * level))
        pieces.append((exchange(far, count, 1), count // 2 + 4 * level + 2))
    return pieces


def slots_of(rows, rows_each, count):
    owner = rows // rows_each
    offset = owner ^ lax.axis_index("dev")
    plane = (offset >> 1) & 3
    swapped = ((plane & 1) << 1) | (plane >> 1)
    label = jnp.where(owner % 2 == 0, plane, swapped)
    slot = (offset & 1) * (count // 2) + (offset >> 3) * 4 + label
    return slot, rows % rows_each


def aperture_kernel(slots, rows_a, rows_b, weights, *refs, aperture, blocks, outs, scale):
    pieces = refs[: len(slots)]
    out_ref, held, left, right, sems = refs[len(slots) :]
    copies = []
    for i, (piece, slot) in enumerate(zip(pieces, slots, strict=True)):
        copies.append(pltpu.make_async_copy(piece, held.at[pl.ds(slot, piece.shape[0])], sems.at[i]))
        copies[-1].start()
    for copy in copies:
        copy.wait()
    lane = lax.broadcasted_iota(jnp.int32, (ROWS, LANES), 1)
    row = lax.broadcasted_iota(jnp.int32, (ROWS, LANES), 0)
    tile = ROWS * blocks

    def shifted(tiles, amount, carried, **how):
        rolled = [pltpu.roll(t, amount, 1, **how) for t in tiles]
        before = [jnp.zeros((ROWS, LANES), jnp.float32)] + rolled[:-1]
        return [jnp.where(carried, b, r) for b, r in zip(before, rolled, strict=True)]

    def columns(ref, p):
        return jnp.concatenate(
            [ref[pl.ds(tile * g + p, ROWS, stride=blocks), :] for g in range(aperture // ROWS)], axis=0
        )

    def one_output(o, lhs_ref, rhs_ref):
        for k in range(aperture):
            here = pl.ds(blocks * k, blocks)
            lhs_ref[here, :] = held[rows_a[o, k]].astype(jnp.float32) * weights[o, k]
            rhs_ref[here, :] = held[rows_b[o, k]].astype(jnp.float32)
        delayed = [columns(rhs_ref, p).astype(jnp.bfloat16) for p in range(blocks)]
        lhs = jnp.concatenate([columns(lhs_ref, p) for p in range(blocks)], axis=0).T
        high = lhs.astype(jnp.bfloat16)
        low = (lhs - high.astype(jnp.float32)).astype(jnp.bfloat16)
        none = jnp.zeros((aperture, LANES), jnp.bfloat16)
        products = []
        for n in range(0, blocks, 2):
            depth = aperture * (n + 2)
            rhs = jnp.concatenate(
                [
                    jnp.concatenate([delayed[n - p] if p <= n else none, delayed[n + 1 - p]], axis=1)
                    for p in range(n + 2)
                ],
                axis=0,
            )
            product = jnp.dot(high[:, :depth], rhs, preferred_element_type=jnp.float32)
            product += jnp.dot(low[:, :depth], rhs, preferred_element_type=jnp.float32)
            products += [product[:, :LANES], product[:, LANES:]]
        total = [q[LANES - ROWS :] for q in products]
        for g in range(LANES // ROWS - 2, -1, -1):
            moved = shifted(total, ROWS, lane < ROWS)
            total = [m + q[ROWS * g : ROWS * g + ROWS] for m, q in zip(moved, products, strict=True)]
        total = shifted(total, 0, lane < row, stride=1, stride_axis=0)
        sums = jnp.concatenate([jnp.sum(t, axis=0, keepdims=True) for t in total], axis=1)
        out_ref[pl.ds(o, 1), :] = sums * scale

    def step(i, carry):
        for u in range(PER_STEP):
            one_output(i * PER_STEP + u, left.at[u], right.at[u])
        return carry

    lax.fori_loop(0, outs // PER_STEP, step, 0)


def aperture_sums(rows_a, rows_b, weights, pieces, rows_each, scale):
    outs, aperture = rows_a.shape
    blocks = pieces[0][0].shape[1]
    held = sum(piece.shape[0] for piece, _ in pieces)
    work = pltpu.VMEM((PER_STEP, aperture * blocks, LANES), jnp.float32)
    return pl.pallas_call(
        functools.partial(
            aperture_kernel,
            [slot * rows_each for _, slot in pieces],
            aperture=aperture,
            blocks=blocks,
            outs=outs,
            scale=scale,
        ),
        out_shape=jax.ShapeDtypeStruct((outs, blocks * LANES), jnp.float32),
        in_specs=[pl.BlockSpec(memory_space=pltpu.SMEM)] * 3 + [pl.BlockSpec(memory_space=pl.ANY)] * len(pieces),
        out_specs=pl.BlockSpec(memory_space=pltpu.VMEM),
        scratch_shapes=[
            pltpu.VMEM((held, blocks, LANES), jnp.bfloat16),
            work,
            work,
            pltpu.SemaphoreType.DMA((len(pieces),)),
        ],
        name="aperture_sums",
    )(rows_a, rows_b, weights, *[piece for piece, _ in pieces])


def shards(traces, fetch_rows, pair_left, pair_right, taper_index, taper_table):
    rows_each, samples = traces.shape
    count = lax.axis_size("dev")
    outputs, aperture = pair_left.shape[1:]
    pieces = gather_blocks(traces.reshape(rows_each, samples // LANES, LANES), count)

    slot, row = slots_of(fetch_rows[0], rows_each, count)
    table = jnp.stack([slot, row], axis=1).astype(jnp.bfloat16)
    wanted = jnp.concatenate([pair_left[0], pair_right[0]], axis=0).reshape(-1)
    onehot = (wanted[:, None] == jnp.arange(table.shape[0], dtype=jnp.int32)[None, :]).astype(jnp.bfloat16)
    found = jnp.dot(onehot, table, preferred_element_type=jnp.float32).astype(jnp.int32)
    places = (found[:, 0] * rows_each + found[:, 1]).reshape(2, outputs, aperture)
    weights = jnp.zeros((outputs, aperture), jnp.float32)
    for j in range(taper_table.shape[0]):
        weights = jnp.where(taper_index[0] == j, taper_table[j], weights)

    scale = float(1.0 / (samples * aperture * lax.axis_size("group")) ** 0.5)
    partial = aperture_sums(places[0], places[1], weights, pieces, rows_each, scale)
    return lax.psum_scatter(partial, "group", scatter_dimension=1, tiled=True)


def solution(mesh):
    return jax.shard_map(
        shards,
        mesh=mesh,
        in_specs=(
            P(("group", "dev"), None),
            P("group", "dev"),
            P("group", "dev", None),
            P("group", "dev", None),
            P("group", "dev", None),
            P(),
        ),
        out_specs=P("dev", "group"),
        check_vma=False,
    )
```

```python
import functools

import jax
import jax.numpy as jnp
from jax import lax
from jax.experimental import pallas as pl
from jax.experimental.pallas import tpu as pltpu
from jax.sharding import PartitionSpec as P


LANES = 128
ROWS = 8
PER_STEP = 8


def exchange(value, count, even, odd=None):
    odd = even if odd is None else odd
    return lax.ppermute(value, "dev", [(i, i ^ (odd if i & 1 else even)) for i in range(count)])


def gather_blocks(own, count):
    levels = {0: own}
    pieces = []

    def level_of(level):
        if level not in levels:
            low = level & -level
            levels[level] = exchange(level_of(level ^ low), count, 8 * low)
        return levels[level]

    for level in range(count // 8):
        near = exchange(level_of(level), count, 2, 4)
        both = jnp.concatenate([level_of(level), near], axis=0)
        far = exchange(both, count, 4, 2)
        pieces.append((both, 4 * level))
        pieces.append((far, 4 * level + 2))
        pieces.append((exchange(both, count, 1), count // 2 + 4 * level))
        pieces.append((exchange(far, count, 1), count // 2 + 4 * level + 2))
    return pieces


def slots_of(rows, rows_each, count):
    owner = rows // rows_each
    offset = owner ^ lax.axis_index("dev")
    plane = (offset >> 1) & 3
    swapped = ((plane & 1) << 1) | (plane >> 1)
    label = jnp.where(owner % 2 == 0, plane, swapped)
    slot = (offset & 1) * (count // 2) + (offset >> 3) * 4 + label
    return slot, rows % rows_each


def aperture_kernel(slots, places, tapers, table, *refs, aperture, blocks, outs, scale):
    pieces = refs[: len(slots)]
    out_ref, held, left, right, sems = refs[len(slots) :]
    copies = []
    for i, (piece, slot) in enumerate(zip(pieces, slots, strict=True)):
        copies.append(pltpu.make_async_copy(piece, held.at[pl.ds(slot, piece.shape[0])], sems.at[i]))
        copies[-1].start()
    for copy in copies:
        copy.wait()
    lane = lax.broadcasted_iota(jnp.int32, (ROWS, LANES), 1)
    row = lax.broadcasted_iota(jnp.int32, (ROWS, LANES), 0)
    tile = ROWS * blocks

    def shifted(tiles, amount, carried, **how):
        rolled = [pltpu.roll(t, amount, 1, **how) for t in tiles]
        before = [jnp.zeros((ROWS, LANES), jnp.float32)] + rolled[:-1]
        return [jnp.where(carried, b, r) for b, r in zip(before, rolled, strict=True)]

    def columns(ref, p):
        return jnp.concatenate(
            [ref[pl.ds(tile * g + p, ROWS, stride=blocks), :] for g in range(aperture // ROWS)], axis=0
        )

    def one_output(o, lhs_ref, rhs_ref):
        for k in range(aperture):
            here = pl.ds(blocks * k, blocks)
            pair = o * aperture + k
            lhs_ref[here, :] = held[places[0, pair]].astype(jnp.float32) * table[tapers[o, k]]
            rhs_ref[here, :] = held[places[0, outs * aperture + pair]].astype(jnp.float32)
        delayed = [columns(rhs_ref, p).astype(jnp.bfloat16) for p in range(blocks)]
        lhs = jnp.concatenate([columns(lhs_ref, p) for p in range(blocks)], axis=0).T
        high = lhs.astype(jnp.bfloat16)
        low = (lhs - high.astype(jnp.float32)).astype(jnp.bfloat16)
        none = jnp.zeros((aperture, LANES), jnp.bfloat16)
        products = []
        for n in range(0, blocks, 2):
            depth = aperture * (n + 2)
            rhs = jnp.concatenate(
                [
                    jnp.concatenate([delayed[n - p] if p <= n else none, delayed[n + 1 - p]], axis=1)
                    for p in range(n + 2)
                ],
                axis=0,
            )
            product = jnp.dot(high[:, :depth], rhs, preferred_element_type=jnp.float32)
            product += jnp.dot(low[:, :depth], rhs, preferred_element_type=jnp.float32)
            products += [product[:, :LANES], product[:, LANES:]]
        total = [q[LANES - ROWS :] for q in products]
        for g in range(LANES // ROWS - 2, -1, -1):
            moved = shifted(total, ROWS, lane < ROWS)
            total = [m + q[ROWS * g : ROWS * g + ROWS] for m, q in zip(moved, products, strict=True)]
        total = shifted(total, 0, lane < row, stride=1, stride_axis=0)
        sums = jnp.concatenate([jnp.sum(t, axis=0, keepdims=True) for t in total], axis=1)
        out_ref[pl.ds(o, 1), :] = sums * scale

    def step(i, carry):
        for u in range(PER_STEP):
            one_output(i * PER_STEP + u, left.at[u], right.at[u])
        return carry

    lax.fori_loop(0, outs // PER_STEP, step, 0)


def aperture_sums(places, tapers, table, pieces, rows_each, scale):
    outs, aperture = tapers.shape
    blocks = pieces[0][0].shape[1]
    held = sum(piece.shape[0] for piece, _ in pieces)
    work = pltpu.VMEM((PER_STEP, aperture * blocks, LANES), jnp.float32)
    return pl.pallas_call(
        functools.partial(
            aperture_kernel,
            [slot * rows_each for _, slot in pieces],
            aperture=aperture,
            blocks=blocks,
            outs=outs,
            scale=scale,
        ),
        out_shape=jax.ShapeDtypeStruct((outs, blocks * LANES), jnp.float32),
        in_specs=[pl.BlockSpec(memory_space=pltpu.SMEM)] * 3 + [pl.BlockSpec(memory_space=pl.ANY)] * len(pieces),
        out_specs=pl.BlockSpec(memory_space=pltpu.VMEM),
        scratch_shapes=[
            pltpu.VMEM((held, blocks, LANES), jnp.bfloat16),
            work,
            work,
            pltpu.SemaphoreType.DMA((len(pieces),)),
        ],
        name="aperture_sums",
    )(places, tapers, table, *[piece for piece, _ in pieces])


def shards(traces, fetch_rows, pair_left, pair_right, taper_index, taper_table):
    rows_each, samples = traces.shape
    count = lax.axis_size("dev")
    _, aperture = pair_left.shape[1:]
    pieces = gather_blocks(traces.reshape(rows_each, samples // LANES, LANES), count)

    slot, row = slots_of(fetch_rows, rows_each, count)
    digits = jnp.concatenate([slot, row], axis=0).astype(jnp.bfloat16)
    wanted = jnp.concatenate([pair_left.reshape(1, -1), pair_right.reshape(1, -1)], axis=1)
    listed = lax.broadcasted_iota(jnp.int32, (digits.shape[1], wanted.shape[1]), 0)
    found = jnp.dot(digits, (listed == wanted).astype(jnp.bfloat16), preferred_element_type=jnp.float32)
    places = (found[:1] * rows_each + found[1:]).astype(jnp.int32)

    scale = float(1.0 / (samples * aperture * lax.axis_size("group")) ** 0.5)
    partial = aperture_sums(places, taper_index[0], taper_table, pieces, rows_each, scale)
    return lax.psum_scatter(partial, "group", scatter_dimension=1, tiled=True)


def solution(mesh):
    return jax.shard_map(
        shards,
        mesh=mesh,
        in_specs=(
            P(("group", "dev"), None),
            P("group", "dev"),
            P("group", "dev", None),
            P("group", "dev", None),
            P("group", "dev", None),
            P(),
        ),
        out_specs=P("dev", "group"),
        check_vma=False,
    )
```

```python
import functools

import jax
import jax.numpy as jnp
from jax import lax
from jax.experimental import pallas as pl
from jax.experimental.pallas import tpu as pltpu
from jax.sharding import PartitionSpec as P


LANES = 128
ROWS = 8
PER_STEP = 8
WORK_BYTES = 16 << 20


def exchange(value, count, even, odd=None):
    odd = even if odd is None else odd
    return lax.ppermute(value, "dev", [(i, i ^ (odd if i & 1 else even)) for i in range(count)])


def gather_blocks(own, count):
    levels = {0: own}
    pieces = []

    def level_of(level):
        if level not in levels:
            low = level & -level
            levels[level] = exchange(level_of(level ^ low), count, 8 * low)
        return levels[level]

    for level in range(count // 8):
        near = exchange(level_of(level), count, 2, 4)
        both = jnp.concatenate([level_of(level), near], axis=0)
        far = exchange(both, count, 4, 2)
        pieces.append((both, 4 * level))
        pieces.append((far, 4 * level + 2))
        pieces.append((exchange(both, count, 1), count // 2 + 4 * level))
        pieces.append((exchange(far, count, 1), count // 2 + 4 * level + 2))
    return pieces


def slots_of(rows, rows_each, count):
    owner = rows // rows_each
    offset = owner ^ lax.axis_index("dev")
    plane = (offset >> 1) & 3
    swapped = ((plane & 1) << 1) | (plane >> 1)
    label = jnp.where(owner % 2 == 0, plane, swapped)
    slot = (offset & 1) * (count // 2) + (offset >> 3) * 4 + label
    return slot, rows % rows_each


def aperture_kernel(slots, places, tapers, table, *refs, aperture, blocks, outs, scale):
    pieces = refs[: len(slots)]
    out_ref, held, left, right, weights, sems = refs[len(slots) :]
    copies = []
    for i, (piece, slot) in enumerate(zip(pieces, slots, strict=True)):
        copies.append(pltpu.make_async_copy(piece, held.at[pl.ds(slot, piece.shape[0])], sems.at[i]))
        copies[-1].start()
    lane = lax.broadcasted_iota(jnp.int32, (ROWS, LANES), 1)
    row = lax.broadcasted_iota(jnp.int32, (ROWS, LANES), 0)
    tile = ROWS * blocks
    half = LANES // 2
    index = tapers[...]
    chosen = jnp.zeros(index.shape, jnp.float32)
    for j in range(table.shape[0]):
        chosen = jnp.where(index == j, table[j], chosen)
    weights[...] = jnp.concatenate([chosen] * blocks, axis=1)
    for copy in copies:
        copy.wait()

    def shifted(tiles, amount, carried, **how):
        rolled = [pltpu.roll(t, amount, 1, **how) for t in tiles]
        before = [jnp.zeros((ROWS, LANES), jnp.float32)] + rolled[:-1]
        return [jnp.where(carried, b, r) for b, r in zip(before, rolled, strict=True)]

    def columns(ref, p):
        parts = [ref[pl.ds(tile * g + p, ROWS, stride=blocks), :] for g in range(aperture // ROWS)]
        return jnp.concatenate(parts, axis=0).astype(jnp.bfloat16)

    def toeplitz(source, n, depth):
        none = jnp.zeros((aperture, LANES), jnp.bfloat16)
        pick = lambda i: source[i] if i >= 0 else none
        rows = [jnp.concatenate([pick(n - p), pick(n + 1 - p)], axis=1) for p in range(depth)]
        return jnp.concatenate(rows, axis=0)

    def one_output(o, left_ref, right_ref):
        for k in range(aperture):
            here = pl.ds(blocks * k, blocks)
            pair = o * aperture + k
            left_ref[here, :] = held[places[0, pair]].astype(jnp.float32)
            right_ref[here, :] = held[places[0, outs * aperture + pair]].astype(jnp.float32)
        even = [columns(right_ref, p) for p in range(blocks)]
        late = jnp.concatenate(
            [jnp.zeros((aperture, half), jnp.bfloat16), jnp.concatenate(even, axis=1)[:, :-half]], axis=1
        )
        odd = [late[:, LANES * p : LANES * (p + 1)] for p in range(blocks)]
        lhs = jnp.concatenate([columns(left_ref, p) for p in range(blocks)], axis=0).T
        lhs = lhs.astype(jnp.float32) * weights[pl.ds(o, 1), :]
        high = lhs.astype(jnp.bfloat16)
        low = (lhs - high.astype(jnp.float32)).astype(jnp.bfloat16)
        products = []
        for n in range(0, blocks, 2):
            depth = blocks // 2 if n + 2 <= blocks // 2 else blocks
            wide = depth * aperture
            factor = jnp.concatenate(
                [jnp.concatenate([term[:half, :wide], term[half:, :wide]], axis=1) for term in (high, low)], axis=0
            )
            delayed = jnp.concatenate([toeplitz(even, n, depth), toeplitz(odd, n, depth)], axis=0)
            both = jnp.dot(factor, delayed, preferred_element_type=jnp.float32)
            both = both[:half] + both[half:]
            products += [both[:, :LANES], both[:, LANES:]]
        total = [q[half - ROWS :] for q in products]
        for g in range(half // ROWS - 2, -1, -1):
            moved = shifted(total, ROWS, lane < ROWS)
            total = [m + q[ROWS * g : ROWS * g + ROWS] for m, q in zip(moved, products, strict=True)]
        total = shifted(total, 0, lane < row, stride=1, stride_axis=0)
        sums = jnp.concatenate([jnp.sum(t, axis=0, keepdims=True) for t in total], axis=1)
        out_ref[pl.ds(o, 1), :] = sums * scale

    def step(i, carry):
        for u in range(PER_STEP):
            one_output(i * PER_STEP + u, left.at[u], right.at[u])
        return carry

    lax.fori_loop(0, outs // PER_STEP, step, 0)


def aperture_sums(places, tapers, table, pieces, rows_each, scale):
    outs, aperture = tapers.shape
    blocks = pieces[0][0].shape[1]
    held = sum(piece.shape[0] for piece, _ in pieces)
    work = pltpu.VMEM((PER_STEP, aperture * blocks, LANES), jnp.float32)
    scalars, vectors = pl.BlockSpec(memory_space=pltpu.SMEM), pl.BlockSpec(memory_space=pltpu.VMEM)
    held_bytes = held * blocks * LANES * 2
    return pl.pallas_call(
        functools.partial(
            aperture_kernel,
            [slot * rows_each for _, slot in pieces],
            aperture=aperture,
            blocks=blocks,
            outs=outs,
            scale=scale,
        ),
        out_shape=jax.ShapeDtypeStruct((outs, blocks * LANES), jnp.float32),
        in_specs=[scalars, vectors, scalars] + [pl.BlockSpec(memory_space=pl.ANY)] * len(pieces),
        out_specs=vectors,
        scratch_shapes=[
            pltpu.VMEM((held, blocks, LANES), jnp.bfloat16),
            work,
            work,
            pltpu.VMEM((outs, aperture * blocks), jnp.float32),
            pltpu.SemaphoreType.DMA((len(pieces),)),
        ],
        compiler_params=pltpu.CompilerParams(vmem_limit_bytes=held_bytes + WORK_BYTES),
        name="aperture_sums",
    )(places, tapers, table, *[piece for piece, _ in pieces])


def shards(traces, fetch_rows, pair_left, pair_right, taper_index, taper_table):
    rows_each, samples = traces.shape
    count = lax.axis_size("dev")
    _, aperture = pair_left.shape[1:]
    pieces = gather_blocks(traces.reshape(rows_each, samples // LANES, LANES), count)

    slot, row = slots_of(fetch_rows, rows_each, count)
    digits = jnp.concatenate([slot, row], axis=0).astype(jnp.bfloat16)
    wanted = jnp.concatenate([pair_left.reshape(1, -1), pair_right.reshape(1, -1)], axis=1)
    listed = lax.broadcasted_iota(jnp.int32, (digits.shape[1], wanted.shape[1]), 0)
    found = jnp.dot(digits, (listed == wanted).astype(jnp.bfloat16), preferred_element_type=jnp.float32)
    places = (found[:1] * rows_each + found[1:]).astype(jnp.int32)

    scale = float(1.0 / (samples * aperture * lax.axis_size("group")) ** 0.5)
    partial = aperture_sums(places, taper_index[0], taper_table, pieces, rows_each, scale)
    return lax.psum_scatter(partial, "group", scatter_dimension=1, tiled=True)


def solution(mesh):
    return jax.shard_map(
        shards,
        mesh=mesh,
        in_specs=(
            P(("group", "dev"), None),
            P("group", "dev"),
            P("group", "dev", None),
            P("group", "dev", None),
            P("group", "dev", None),
            P(),
        ),
        out_specs=P("dev", "group"),
        check_vma=False,
    )
```

```python
import functools

import jax
import jax.numpy as jnp
from jax import lax
from jax.experimental import pallas as pl
from jax.experimental.pallas import tpu as pltpu
from jax.sharding import PartitionSpec as P


LANES = 128
ROWS = 8
PER_STEP = 4
WORK_BYTES = 16 << 20


def exchange(value, count, even, odd=None):
    odd = even if odd is None else odd
    return lax.ppermute(value, "dev", [(i, i ^ (odd if i & 1 else even)) for i in range(count)])


def gather_blocks(own, count):
    levels = {0: own}
    fars = []
    pieces = []

    def level_of(level):
        if level not in levels:
            low = level & -level
            levels[level] = exchange(level_of(level ^ low), count, 8 * low)
        return levels[level]

    for level in range(count // 8):
        near = exchange(level_of(level), count, 2, 4)
        both = jnp.concatenate([level_of(level), near], axis=0)
        far = exchange(fars[0], count, 8) if level == 1 else exchange(both, count, 4, 2)
        fars.append(far)
        pieces.append((both, 4 * level))
        pieces.append((far, 4 * level + 2))
        pieces.append((exchange(both, count, 1), count // 2 + 4 * level))
        pieces.append((exchange(far, count, 1), count // 2 + 4 * level + 2))
    return pieces


def slots_of(rows, rows_each, count):
    owner = rows // rows_each
    offset = owner ^ lax.axis_index("dev")
    plane = (offset >> 1) & 3
    swapped = ((plane & 1) << 1) | (plane >> 1)
    label = jnp.where(owner % 2 == 0, plane, swapped)
    slot = (offset & 1) * (count // 2) + (offset >> 3) * 4 + label
    return slot, rows % rows_each


def aperture_kernel(slots, places, tapers, table, *refs, aperture, blocks, outs, scale):
    pieces = refs[: len(slots)]
    out_ref, held, left, right, products, weights, sems = refs[len(slots) :]
    copies = []
    for i, (piece, slot) in enumerate(zip(pieces, slots, strict=True)):
        copies.append(pltpu.make_async_copy(piece, held.at[pl.ds(slot, piece.shape[0])], sems.at[i]))
        copies[-1].start()
    lane = lax.broadcasted_iota(jnp.int32, (ROWS, LANES), 1)
    row = lax.broadcasted_iota(jnp.int32, (ROWS, LANES), 0)
    tile = ROWS * blocks
    half = LANES // 2
    index = tapers[...]
    chosen = jnp.zeros(index.shape, jnp.float32)
    for j in range(table.shape[0]):
        chosen = jnp.where(index == j, table[j], chosen)
    weights[...] = jnp.concatenate([chosen] * blocks, axis=1)
    for copy in copies:
        copy.wait()

    def shifted(tiles, amount, carried, **how):
        rolled = [pltpu.roll(t, amount, 1, **how) for t in tiles]
        before = [jnp.zeros((ROWS, LANES), jnp.float32)] + rolled[:-1]
        return [jnp.where(carried, b, r) for b, r in zip(before, rolled, strict=True)]

    def columns(ref, p):
        parts = [ref[pl.ds(tile * g + p, ROWS, stride=blocks), :] for g in range(aperture // ROWS)]
        return jnp.concatenate(parts, axis=0).astype(jnp.bfloat16)

    def toeplitz(source, n, depth):
        none = jnp.zeros((aperture, LANES), jnp.bfloat16)
        pick = lambda i: source[i] if i >= 0 else none
        rows = [jnp.concatenate([pick(n - p), pick(n + 1 - p)], axis=1) for p in range(depth)]
        return jnp.concatenate(rows, axis=0)

    def multiply(o, left_ref, right_ref, product_ref):
        left_places = places.at[0, pl.ds(o * aperture, aperture)]
        right_places = places.at[0, pl.ds((outs + o) * aperture, aperture)]
        for k in range(aperture):
            here = pl.ds(blocks * k, blocks)
            left_ref[here, :] = held[left_places[k]].astype(jnp.float32)
            right_ref[here, :] = held[right_places[k]].astype(jnp.float32)
        even = [columns(right_ref, p) for p in range(blocks)]
        late = jnp.concatenate(
            [jnp.zeros((aperture, half), jnp.bfloat16), jnp.concatenate(even, axis=1)[:, :-half]], axis=1
        )
        odd = [late[:, LANES * p : LANES * (p + 1)] for p in range(blocks)]
        lhs = jnp.concatenate([columns(left_ref, p) for p in range(blocks)], axis=0).T
        lhs = lhs.astype(jnp.float32) * weights[pl.ds(o, 1), :]
        high = lhs.astype(jnp.bfloat16)
        low = (lhs - high.astype(jnp.float32)).astype(jnp.bfloat16)
        for n in range(0, blocks, 2):
            depth = blocks // 2 if n + 2 <= blocks // 2 else blocks
            wide = depth * aperture
            factor = jnp.concatenate(
                [jnp.concatenate([term[:half, :wide], term[half:, :wide]], axis=1) for term in (high, low)], axis=0
            )
            delayed = jnp.concatenate([toeplitz(even, n, depth), toeplitz(odd, n, depth)], axis=0)
            both = jnp.dot(factor, delayed, preferred_element_type=jnp.float32)
            product_ref[:, pl.ds(n * LANES, 2 * LANES)] = both[:half] + both[half:]

    def add_up(o, product_ref):
        def tiles(g):
            return [product_ref[pl.ds(ROWS * g, ROWS), pl.ds(v * LANES, LANES)] for v in range(blocks)]

        total = tiles(half // ROWS - 1)
        for g in range(half // ROWS - 2, -1, -1):
            moved = shifted(total, ROWS, lane < ROWS)
            total = [m + t for m, t in zip(moved, tiles(g), strict=True)]
        total = shifted(total, 0, lane < row, stride=1, stride_axis=0)
        sums = jnp.concatenate([jnp.sum(t, axis=0, keepdims=True) for t in total], axis=1)
        out_ref[pl.ds(o, 1), :] = sums * scale

    def multiply_all(i):
        for u in range(PER_STEP):
            multiply(i * PER_STEP + u, left.at[u], right.at[u], products.at[u])

    def add_up_all(i):
        for u in range(PER_STEP):
            add_up(i * PER_STEP + u, products.at[u])

    def step(i, carry):
        add_up_all(i - 1)
        multiply_all(i)
        return carry

    multiply_all(0)
    lax.fori_loop(1, outs // PER_STEP, step, 0)
    add_up_all(outs // PER_STEP - 1)


def aperture_sums(places, tapers, table, pieces, rows_each, scale):
    outs, aperture = tapers.shape
    blocks = pieces[0][0].shape[1]
    held = sum(piece.shape[0] for piece, _ in pieces)
    work = pltpu.VMEM((PER_STEP, aperture * blocks, LANES), jnp.float32)
    scalars, vectors = pl.BlockSpec(memory_space=pltpu.SMEM), pl.BlockSpec(memory_space=pltpu.VMEM)
    held_bytes = held * blocks * LANES * 2
    return pl.pallas_call(
        functools.partial(
            aperture_kernel,
            [slot * rows_each for _, slot in pieces],
            aperture=aperture,
            blocks=blocks,
            outs=outs,
            scale=scale,
        ),
        out_shape=jax.ShapeDtypeStruct((outs, blocks * LANES), jnp.float32),
        in_specs=[scalars, vectors, scalars] + [pl.BlockSpec(memory_space=pl.ANY)] * len(pieces),
        out_specs=vectors,
        scratch_shapes=[
            pltpu.VMEM((held, blocks, LANES), jnp.bfloat16),
            work,
            work,
            pltpu.VMEM((PER_STEP, LANES // 2, blocks * LANES), jnp.float32),
            pltpu.VMEM((outs, aperture * blocks), jnp.float32),
            pltpu.SemaphoreType.DMA((len(pieces),)),
        ],
        compiler_params=pltpu.CompilerParams(vmem_limit_bytes=held_bytes + WORK_BYTES),
        name="aperture_sums",
    )(places, tapers, table, *[piece for piece, _ in pieces])


def shards(traces, fetch_rows, pair_left, pair_right, taper_index, taper_table):
    rows_each, samples = traces.shape
    count = lax.axis_size("dev")
    _, aperture = pair_left.shape[1:]
    pieces = gather_blocks(traces.reshape(rows_each, samples // LANES, LANES), count)

    slot, row = slots_of(fetch_rows, rows_each, count)
    digits = jnp.concatenate([slot, row], axis=0).astype(jnp.bfloat16)
    wanted = jnp.concatenate([pair_left.reshape(1, -1), pair_right.reshape(1, -1)], axis=1)
    listed = lax.broadcasted_iota(jnp.int32, (digits.shape[1], wanted.shape[1]), 0)
    found = jnp.dot(digits, (listed == wanted).astype(jnp.bfloat16), preferred_element_type=jnp.float32)
    places = (found[:1] * rows_each + found[1:]).astype(jnp.int32)

    scale = float(1.0 / (samples * aperture * lax.axis_size("group")) ** 0.5)
    partial = aperture_sums(places, taper_index[0], taper_table, pieces, rows_each, scale)
    return lax.psum_scatter(partial, "group", scatter_dimension=1, tiled=True)


def solution(mesh):
    return jax.shard_map(
        shards,
        mesh=mesh,
        in_specs=(
            P(("group", "dev"), None),
            P("group", "dev"),
            P("group", "dev", None),
            P("group", "dev", None),
            P("group", "dev", None),
            P(),
        ),
        out_specs=P("dev", "group"),
        check_vma=False,
    )
```

```python
import functools

import jax
import jax.numpy as jnp
from jax import lax
from jax.experimental import pallas as pl
from jax.experimental.pallas import tpu as pltpu
from jax.sharding import PartitionSpec as P


LANES = 128
ROWS = 8
PER_STEP = 4
WORK_BYTES = 16 << 20


def exchange(value, count, even, odd=None):
    odd = even if odd is None else odd
    return lax.ppermute(value, "dev", [(i, i ^ (odd if i & 1 else even)) for i in range(count)])


def tiles_of(rows):
    return rows.reshape(rows.shape[0], rows.shape[1] // LANES, LANES)


def gather_blocks(traces, count):
    rows = {0: traces}
    levels = {}
    fars = []
    pieces = []

    def rows_of(level):
        if level not in rows:
            low = level & -level
            rows[level] = exchange(rows_of(level ^ low), count, 8 * low)
        return rows[level]

    def level_of(level):
        if level not in levels:
            levels[level] = exchange(level_of(0), count, 8) if level == 1 else tiles_of(rows_of(level))
        return levels[level]

    for level in range(count // 8):
        near = exchange(level_of(level), count, 2, 4)
        both = jnp.concatenate([level_of(level), near], axis=0)
        far = exchange(fars[0], count, 8) if level == 1 else exchange(both, count, 4, 2)
        fars.append(far)
        pieces.append((both, 4 * level))
        pieces.append((far, 4 * level + 2))
        pieces.append((exchange(both, count, 1), count // 2 + 4 * level))
        pieces.append((exchange(far, count, 1), count // 2 + 4 * level + 2))
    return pieces


def slots_of(rows, rows_each, count):
    owner = rows // rows_each
    offset = owner ^ lax.axis_index("dev")
    plane = (offset >> 1) & 3
    swapped = ((plane & 1) << 1) | (plane >> 1)
    label = jnp.where(owner % 2 == 0, plane, swapped)
    slot = (offset & 1) * (count // 2) + (offset >> 3) * 4 + label
    return slot, rows % rows_each


def aperture_kernel(slots, places, tapers, table, *refs, aperture, blocks, outs, scale):
    pieces = refs[: len(slots)]
    out_ref, held, left, right, products, weights, sems = refs[len(slots) :]
    copies = []
    for i, (piece, slot) in enumerate(zip(pieces, slots, strict=True)):
        copies.append(pltpu.make_async_copy(piece, held.at[pl.ds(slot, piece.shape[0])], sems.at[i]))
        copies[-1].start()
    lane = lax.broadcasted_iota(jnp.int32, (ROWS, LANES), 1)
    row = lax.broadcasted_iota(jnp.int32, (ROWS, LANES), 0)
    tile = ROWS * blocks
    half = LANES // 2
    index = tapers[...]
    chosen = jnp.zeros(index.shape, jnp.float32)
    for j in range(table.shape[0]):
        chosen = jnp.where(index == j, table[j], chosen)
    weights[...] = jnp.concatenate([chosen] * blocks, axis=1)
    for copy in copies:
        copy.wait()

    def shifted(tiles, amount, carried, **how):
        rolled = [pltpu.roll(t, amount, 1, **how) for t in tiles]
        before = [jnp.zeros((ROWS, LANES), jnp.float32)] + rolled[:-1]
        return [jnp.where(carried, b, r) for b, r in zip(before, rolled, strict=True)]

    def columns(ref, p):
        parts = [ref[pl.ds(tile * g + p, ROWS, stride=blocks), :] for g in range(aperture // ROWS)]
        return jnp.concatenate(parts, axis=0).astype(jnp.bfloat16)

    def toeplitz(source, n, depth):
        none = jnp.zeros((aperture, LANES), jnp.bfloat16)
        pick = lambda i: source[i] if i >= 0 else none
        rows = [jnp.concatenate([pick(n - p), pick(n + 1 - p)], axis=1) for p in range(depth)]
        return jnp.concatenate(rows, axis=0)

    def multiply(o, left_ref, right_ref, product_ref):
        left_places = places.at[0, pl.ds(o * aperture, aperture)]
        right_places = places.at[0, pl.ds((outs + o) * aperture, aperture)]
        for k in range(aperture):
            here = pl.ds(blocks * k, blocks)
            left_ref[here, :] = held[left_places[k]].astype(jnp.float32)
            right_ref[here, :] = held[right_places[k]].astype(jnp.float32)
        even = [columns(right_ref, p) for p in range(blocks)]
        late = jnp.concatenate(
            [jnp.zeros((aperture, half), jnp.bfloat16), jnp.concatenate(even, axis=1)[:, :-half]], axis=1
        )
        odd = [late[:, LANES * p : LANES * (p + 1)] for p in range(blocks)]
        lhs = jnp.concatenate([columns(left_ref, p) for p in range(blocks)], axis=0).T
        lhs = lhs.astype(jnp.float32) * weights[pl.ds(o, 1), :]
        high = lhs.astype(jnp.bfloat16)
        low = (lhs - high.astype(jnp.float32)).astype(jnp.bfloat16)
        for n in range(0, blocks, 2):
            depth = blocks // 2 if n + 2 <= blocks // 2 else blocks
            wide = depth * aperture
            factor = jnp.concatenate(
                [jnp.concatenate([term[:half, :wide], term[half:, :wide]], axis=1) for term in (high, low)], axis=0
            )
            delayed = jnp.concatenate([toeplitz(even, n, depth), toeplitz(odd, n, depth)], axis=0)
            both = jnp.dot(factor, delayed, preferred_element_type=jnp.float32)
            product_ref[:, pl.ds(n * LANES, 2 * LANES)] = both[:half] + both[half:]

    def add_up(o, product_ref):
        def tiles(g):
            return [product_ref[pl.ds(ROWS * g, ROWS), pl.ds(v * LANES, LANES)] for v in range(blocks)]

        total = tiles(half // ROWS - 1)
        for g in range(half // ROWS - 2, -1, -1):
            moved = shifted(total, ROWS, lane < ROWS)
            total = [m + t for m, t in zip(moved, tiles(g), strict=True)]
        total = shifted(total, 0, lane < row, stride=1, stride_axis=0)
        sums = jnp.concatenate([jnp.sum(t, axis=0, keepdims=True) for t in total], axis=1)
        out_ref[pl.ds(o, 1), :] = sums * scale

    def multiply_all(i):
        for u in range(PER_STEP):
            multiply(i * PER_STEP + u, left.at[u], right.at[u], products.at[u])

    def add_up_all(i):
        for u in range(PER_STEP):
            add_up(i * PER_STEP + u, products.at[u])

    def step(i, carry):
        add_up_all(i - 1)
        multiply_all(i)
        return carry

    multiply_all(0)
    lax.fori_loop(1, outs // PER_STEP, step, 0)
    add_up_all(outs // PER_STEP - 1)


def aperture_sums(places, tapers, table, pieces, rows_each, scale):
    outs, aperture = tapers.shape
    blocks = pieces[0][0].shape[1]
    held = sum(piece.shape[0] for piece, _ in pieces)
    work = pltpu.VMEM((PER_STEP, aperture * blocks, LANES), jnp.float32)
    scalars, vectors = pl.BlockSpec(memory_space=pltpu.SMEM), pl.BlockSpec(memory_space=pltpu.VMEM)
    held_bytes = held * blocks * LANES * 2
    return pl.pallas_call(
        functools.partial(
            aperture_kernel,
            [slot * rows_each for _, slot in pieces],
            aperture=aperture,
            blocks=blocks,
            outs=outs,
            scale=scale,
        ),
        out_shape=jax.ShapeDtypeStruct((outs, blocks * LANES), jnp.float32),
        in_specs=[scalars, vectors, scalars] + [pl.BlockSpec(memory_space=pl.ANY)] * len(pieces),
        out_specs=vectors,
        scratch_shapes=[
            pltpu.VMEM((held, blocks, LANES), jnp.bfloat16),
            work,
            work,
            pltpu.VMEM((PER_STEP, LANES // 2, blocks * LANES), jnp.float32),
            pltpu.VMEM((outs, aperture * blocks), jnp.float32),
            pltpu.SemaphoreType.DMA((len(pieces),)),
        ],
        compiler_params=pltpu.CompilerParams(vmem_limit_bytes=held_bytes + WORK_BYTES),
        name="aperture_sums",
    )(places, tapers, table, *[piece for piece, _ in pieces])


def shards(traces, fetch_rows, pair_left, pair_right, taper_index, taper_table):
    rows_each, samples = traces.shape
    count = lax.axis_size("dev")
    _, aperture = pair_left.shape[1:]
    pieces = gather_blocks(traces, count)

    slot, row = slots_of(fetch_rows, rows_each, count)
    digits = jnp.concatenate([slot, row], axis=0).astype(jnp.bfloat16)
    wanted = jnp.concatenate([pair_left.reshape(1, -1), pair_right.reshape(1, -1)], axis=1)
    listed = lax.broadcasted_iota(jnp.int32, (digits.shape[1], wanted.shape[1]), 0)
    found = jnp.dot(digits, (listed == wanted).astype(jnp.bfloat16), preferred_element_type=jnp.float32)
    places = (found[:1] * rows_each + found[1:]).astype(jnp.int32)

    scale = float(1.0 / (samples * aperture * lax.axis_size("group")) ** 0.5)
    partial = aperture_sums(places, taper_index[0], taper_table, pieces, rows_each, scale)
    return lax.psum_scatter(partial, "group", scatter_dimension=1, tiled=True)


def solution(mesh):
    return jax.shard_map(
        shards,
        mesh=mesh,
        in_specs=(
            P(("group", "dev"), None),
            P("group", "dev"),
            P("group", "dev", None),
            P("group", "dev", None),
            P("group", "dev", None),
            P(),
        ),
        out_specs=P("dev", "group"),
        check_vma=False,
    )
```
